128 devices in a mesh: gx: 16 (over x, y), gy: 8 (over z, core).
Axes of the slice: x: 4, y: 4, z: 4, core: 2. Of those that a mesh axis runs over, the one named last changes fastest.
Arguments:
- head: float32 [512, 384, 128], P('gx', 'gy'), may hold values from -6 to 6
- conductivity: float32 [512, 384, 128], P('gx', 'gy'), may hold values from 0.1 to 10
- storage: float32 [512, 384, 128], P('gx', 'gy'), may hold values from 0.3 to 3
- recharge: float32 [512, 384, 128], P('gx', 'gy'), may hold values from -6 to 6
- misfit: float32 [512, 384, 128], P('gx', 'gy'), may hold values from -6 to 6
- reservoir_cell: int32 [2048], P(('gx', 'gy')), may hold values from 0 to 196607
- pumping: float32 [2048], P(('gx', 'gy')), may hold values from -25 to 25
- observed: float32 [2048], P(('gx', 'gy')), may hold values from -25 to 25
- tile_owner: int32 [12288, 1], P(('gx', 'gy')), may hold values from 0 to 127; in each aligned block of 96 rows (0 to 95, 96 to 191, ...) at most 2 rows name the same one
- tile_inverse: bfloat16 [32768, 128, 128], P(('gx', 'gy')), may hold values from -0.01 to 0.05
- zone_of_column: int32 [512, 384], P('gx', 'gy'), may hold values from 0 to 49151
Outputs:
- new_head: float32 [512, 384, 128], P('gx', 'gy')
- zone_gradient: float32 [49152], P(('gx', 'gy'))
The draws below stay inside these ranges and needn't reach their ends.
Inputs may be any that keep to these rules, and one draw needn't show every extreme that they name: `tile_owner`: in each device's block of 96 tiles no owner is named by more than 2 tiles. `reservoir_cell`: A flat index into the 32 x 48 x 128 block of the device that holds the reservoir.
All inputs are finite; a program needn't handle non-finite values.
Results may differ from the reference program's by a relative error of at most 0.0016.
Values may be sent and summed in bfloat16 or wider, within the bound.
A program may use at most 128 MiB of HBM per device.

```python
import math
import jax
import jax.numpy as jnp
import numpy as np
from jax import lax

CX = 32
CY = 48
CZ = 128
AGG = 4
CYCLES = 2
SWEEPS = 2
RES_DEV = 16
NX = 512
NY = 384
TILES_DEV = 96
MOST = 2
NTILES = 12288
INV_SLOTS = 32768
RESERVOIRS = 2048
ZONES = 49152
N_GX = 16
N_GY = 8


def draw_tile_inverse(key, part):
    key_off, key_diag = jax.random.split(jax.random.fold_in(key, 17))
    off_part = jax.random.truncated_normal(key_off, -3.0, 3.0, (INV_SLOTS, CZ, CZ), jnp.float32)
    off_part = off_part * (0.5 / math.sqrt(CZ))
    diag_part = jnp.exp(jax.random.uniform(key_diag, (INV_SLOTS, CZ, 1), jnp.float32, math.log(0.5), math.log(2.0)))
    identity = jnp.eye(CZ, dtype=jnp.float32)
    return (0.02 * (off_part + identity * diag_part)).astype(jnp.bfloat16)


def with_ends(values, key, least, largest):
    spot = [jax.random.randint(jax.random.fold_in(key, axis), (), 0, length) for axis, length in enumerate(values.shape)]
    main_axis = values.shape.index(max(values.shape))
    beside = spot[:main_axis] + [(spot[main_axis] + 1) % values.shape[main_axis]] + spot[main_axis + 1:]
    return values.at[tuple(spot)].set(least).at[tuple(beside)].set(largest)


def block_scale(own_key, shape, cuts, least, high):
    level = 1.0
    for dim, blocks in cuts:
        draws = jax.random.uniform(jax.random.fold_in(jax.random.fold_in(own_key, 6), dim), (blocks,), jnp.float32, least / len(cuts), high / len(cuts))
        level = level * jnp.repeat(jnp.exp(draws), shape[dim] // blocks).reshape((-1,) + (1,) * (len(shape) - 1 - dim))
    return level


def rank_table(number_of, lean):
    portions = [(1 << 20) // math.isqrt(rank ** lean) + 1 for rank in range(1, number_of + 1)]
    scale = 1 + sum(portions) // (1 << 30)
    return np.cumsum(np.array([max(1, weight // scale) for weight in portions]))


def skewed_ids(own_key, dims, count, skew):
    grid = rank_table(count, skew)
    pick = jax.random.randint(jax.random.fold_in(own_key, 1), dims, 0, int(grid[count - 1]))
    grade = jnp.searchsorted(jnp.asarray(grid, jnp.int32), pick, side="right")
    return jax.random.permutation(jax.random.fold_in(own_key, 2), count)[grade].astype(jnp.int32)


def shared_out(key, own, number, rows, number_of, top, limit, lean):
    sequence = jax.random.permutation(key, number_of)
    packed, common = portions_of(number_of, rows * top, limit, lean, True), portions_of(number_of, rows * top, limit, lean, False)
    places = jnp.arange(number_of)

    def named(sizes, turn):
        used = int((sizes > 0).sum())
        fixed = max(1, used // 4)
        moved = fixed + (places - fixed + turn * (used - fixed)) % max(1, number_of - fixed)
        return jnp.zeros((number_of,), jnp.int32).at[sequence[jnp.where(places < fixed, places, moved)]].set(jnp.asarray(sizes, jnp.int32))

    sizes = jnp.where(number % 4 == 0, named(packed, number // 4), named(common, number - number // 4 - 1))
    mixed = jax.random.permutation(jax.random.fold_in(own, 3), number_of)
    source_of, taker = mixed[0:number_of // 2 * 2:2], mixed[1:number_of // 2 * 2:2]
    margin = jnp.minimum(sizes[source_of] - 1, limit - sizes[taker]) // 2
    margin = jnp.where((source_of == sequence[0]) | (taker == sequence[0]) | (sizes[taker] == 0), 0, jnp.maximum(margin, 0))
    moved = jax.random.randint(jax.random.fold_in(own, 4), (number_of // 2,), 0, 1 << 20) % (margin + 1)
    sizes = sizes.at[source_of].add(-moved).at[taker].add(moved)
    items = jnp.searchsorted(jnp.cumsum(sizes), jnp.arange(rows * top), side="right").astype(jnp.int32)
    table = items.reshape(top, rows).T
    table = table[jax.random.permutation(jax.random.fold_in(own, 1), rows)]
    turn = jax.random.randint(jax.random.fold_in(own, 2), (rows, 1), 0, top)
    return jnp.take_along_axis(table, (jnp.arange(top)[None, :] + turn) % top, axis=1)


def portions_of(number_of, total, bound, slope, full):
    portions = [(1 << 20) // math.isqrt(grade ** slope) + 1 for grade in range(1, number_of + 1)]
    largest = bound if full else min(bound, max(-(-total // number_of), total * portions[0] // sum(portions)))
    least = 1 if total - largest >= number_of - 1 else 0
    counts, spare = [largest] + [least] * (number_of - 1), total - largest - least * (number_of - 1)
    while spare > 0:
        candidates = [i for i in range(1, number_of) if counts[i] < largest] or [i for i in range(1, number_of) if counts[i] < bound]
        whole, budget = sum([portions[i] for i in candidates]), spare
        for i in candidates:
            addition = min(bound - counts[i], max(1, budget * portions[i] // whole), spare)
            counts[i] = counts[i] + addition
            spare = spare - addition
    return np.array(counts)


def noise(rng, extent, scale, limit, cuts=(), held_as=jnp.bfloat16):
    drawn = scale * jax.random.normal(rng, extent, jnp.float32)
    if cuts:
        drawn = drawn * block_scale(rng, extent, cuts, -0.22, 0.18)
    return jnp.clip(drawn, -limit, limit).astype(held_as)


def setup_inputs(seed: int = 0) -> dict:
    seeds = jax.random.split(jax.random.key(seed), 12)
    head = noise(seeds[0], (NX, NY, CZ), 1.0, 6.0, ((0, 16), (1, 8)), jnp.float32)
    conductivity = jnp.clip(jnp.exp(math.log(10.0) - 4.6051702 * jax.random.uniform(seeds[1], (NX, NY, CZ), jnp.float32) ** block_scale(seeds[1], (NX, NY, CZ), ((0, 16), (1, 8)), -0.2, 0.2)), 0.1, 10.0)
    storage = jnp.clip(jnp.exp(math.log(3.0) - 2.3025851 * jax.random.uniform(seeds[2], (NX, NY, CZ), jnp.float32) ** block_scale(seeds[2], (NX, NY, CZ), ((0, 16), (1, 8)), -0.2, 0.2)), 0.3, 3.0)
    recharge = noise(seeds[3], (NX, NY, CZ), 1.0, 6.0, ((0, 16), (1, 8)), jnp.float32)
    misfit = noise(seeds[4], (NX, NY, CZ), 1.0, 6.0, ((0, 16), (1, 8)), jnp.float32)
    reservoir_cell = with_ends(jax.random.randint(seeds[5], (RESERVOIRS,), 0, CX * CY * CZ), jax.random.fold_in(seeds[5], 1), 0, (CX * CY * CZ) - 1).astype(jnp.int32)
    pumping = noise(seeds[6], (RESERVOIRS,), 5.0, 25.0, ((0, 128),), jnp.float32)
    observed = noise(seeds[7], (RESERVOIRS,), 5.0, 25.0, ((0, 128),), jnp.float32)
    tile_owner_keys = jax.random.split(jax.random.fold_in(seeds[8], 1), NTILES // TILES_DEV)
    tile_owner_turns = jax.random.permutation(jax.random.fold_in(seeds[8], 3), NTILES // TILES_DEV)
    tile_owner = jax.vmap(lambda own, number: shared_out(jax.random.fold_in(seeds[8], 2), own, number, TILES_DEV, N_GX * N_GY, 1, MOST, 2))(tile_owner_keys, tile_owner_turns).reshape((NTILES, 1))
    tile_inverse = draw_tile_inverse(jax.random.fold_in(seeds[11], 71), 0)
    zone_of_column = with_ends(skewed_ids(seeds[10], (NX, NY), ZONES, 1), jax.random.fold_in(seeds[10], 3), 0, ZONES - 1).astype(jnp.int32)
    return dict(head=head, conductivity=conductivity, storage=storage, recharge=recharge, misfit=misfit, reservoir_cell=reservoir_cell, pumping=pumping, observed=observed, tile_owner=tile_owner, tile_inverse=tile_inverse, zone_of_column=zone_of_column)


relax = 0.8


def neighbours(padded):
    center = padded[..., 1:-1, 1:-1, :]
    zero = jnp.zeros_like(center[..., :1])
    above = jnp.concatenate([center[..., 1:], zero], axis=-1)
    below = jnp.concatenate([zero, center[..., :-1]], axis=-1)
    return center, [padded[..., 2:, 1:-1, :], padded[..., :-2, 1:-1, :], padded[..., 1:-1, 2:, :], padded[..., 1:-1, :-2, :], above, below]


def conductances(padded_k):
    center, beside_all = neighbours(padded_k)
    return [0.5 * (center + other) for other in beside_all]


def apply_operator(padded, diag_part, conds):
    center, beside_all = neighbours(padded)
    result = diag_part * center
    for face, other in zip(conds, beside_all):
        result = result + face * (center - other)
    return result


def row_total(diag_part, conds):
    total = diag_part
    for face in conds:
        total = total + face
    return total


def face_gradient(padded_head, padded_adjoint):
    head_c, head_n = neighbours(padded_head)
    adj_c, adj_n = neighbours(padded_adjoint)
    grad = jnp.zeros_like(head_c)
    for head_o, adj_o in zip(head_n, adj_n):
        grad = grad - 0.5 * (adj_c - adj_o) * (head_c - head_o)
    return grad


def pad_sides(field):
    widths = [(0, 0)] * (field.ndim - 3) + [(1, 1), (1, 1), (0, 0)]
    return jnp.pad(field, widths)


def reference(head, conductivity, storage, recharge, misfit, reservoir_cell, pumping, observed, tile_owner, tile_inverse, zone_of_column):
    devices = N_GX * N_GY
    tiles_x = CX // AGG
    tiles_y = CY // AGG
    conds = conductances(pad_sides(conductivity))
    total = row_total(storage, conds)

    def place(values):
        number = jnp.arange(RESERVOIRS, dtype=jnp.int32)
        owner_dev = number // RES_DEV
        east = owner_dev // N_GY
        north = owner_dev % N_GY
        cell_x = reservoir_cell // (CY * CZ)
        cell_y = (reservoir_cell // CZ) % CY
        cell_z = reservoir_cell % CZ
        field = jnp.zeros((NX, NY, CZ), jnp.float32)
        return field.at[east * CX + cell_x, north * CY + cell_y, cell_z].add(values)

    applied = apply_operator(pad_sides(head), storage, conds)
    rhs = jnp.stack([recharge + place(pumping) - applied, misfit + place(observed)])
    owners = tile_owner[:, 0].reshape(devices, TILES_DEV)
    order = jnp.arange(TILES_DEV, dtype=jnp.int32)
    same = owners[:, :, None] == owners[:, None, :]
    earlier = order[:, None] > order[None, :]
    rank = jnp.sum(same & earlier[None], axis=2).astype(jnp.int32)
    source = jnp.arange(devices, dtype=jnp.int32)[:, None]
    index = (owners * (devices * MOST) + source * MOST + rank).astype(jnp.int32)

    def sweep(state):
        return state + relax * (rhs - apply_operator(pad_sides(state), storage, conds)) / total

    def coarse(residual):
        sums = residual.reshape(2, NX // AGG, AGG, NY // AGG, AGG, CZ).sum(axis=(2, 4))
        grouped = jnp.transpose(sums.reshape(2, N_GX, tiles_x, N_GY, tiles_y, CZ), (1, 3, 2, 4, 0, 5))
        grouped = grouped.reshape(devices, TILES_DEV, 2, CZ).astype(jnp.bfloat16)

        def one_device(pair):
            rows, block = pair
            mats = tile_inverse[rows].astype(jnp.float32)
            return jnp.einsum("tij,tfj->tfi", mats, block.astype(jnp.float32))

        solved = lax.map(one_device, (index, grouped))
        spread = jnp.transpose(solved.reshape(N_GX, N_GY, tiles_x, tiles_y, 2, CZ), (4, 0, 2, 1, 3, 5))
        spread = spread.reshape(2, NX // AGG, NY // AGG, CZ)
        return jnp.repeat(jnp.repeat(spread, AGG, axis=1), AGG, axis=2)

    state = jnp.zeros_like(rhs)
    for cycle in range(CYCLES):
        for step in range(SWEEPS):
            state = sweep(state)
        state = state + coarse(rhs - apply_operator(pad_sides(state), storage, conds))
        for step in range(SWEEPS):
            state = sweep(state)
    new_head = head + state[0]
    grad = face_gradient(pad_sides(new_head), pad_sides(state[1]))
    column = jnp.sum(grad, axis=-1) / CZ
    zone_gradient = jax.ops.segment_sum(column.reshape(-1), zone_of_column.reshape(-1), num_segments=ZONES)
    return new_head, zone_gradient
```

```python
import jax
import jax.numpy as jnp
from jax import lax
from jax.sharding import PartitionSpec as P

AGG = 4
CYCLES = 2
SWEEPS = 2
ZONES_DEV = 384


relax = 0.8


def faces(value):
    result = []
    for axis, dim in (("gx", value.ndim - 3), ("gy", value.ndim - 2)):
        count, length = (lax.axis_size(axis), value.shape[dim])
        up = [(i, (i + 1) % count) for i in range(count - 1)]
        down = [(j, i) for i, j in up]
        last = lax.slice_in_dim(value, length - 1, length, axis=dim)
        initial = lax.slice_in_dim(value, 0, 1, axis=dim)
        result.append((lax.ppermute(last, axis, up), lax.ppermute(initial, axis, down), dim))
    return result


def neighbours(parts):
    center, sides = parts
    beside = []
    for before, after, dim in sides:
        length = center.shape[dim]
        beside.append(jnp.concatenate([lax.slice_in_dim(center, 1, length, axis=dim), after], axis=dim))
        beside.append(jnp.concatenate([before, lax.slice_in_dim(center, 0, length - 1, axis=dim)], axis=dim))
    zero = jnp.zeros_like(center[..., :1])
    above = jnp.concatenate([center[..., 1:], zero], axis=-1)
    below = jnp.concatenate([zero, center[..., :-1]], axis=-1)
    return center, beside + [above, below]


def extended(value):
    return value, faces(value)


def part(parts, i):
    center, sides = parts
    return center[i], [(b[i], a[i], d - 1) for b, a, d in sides]


def conductances(padded_k):
    center, beside_all = neighbours(padded_k)
    return [0.5 * (center + other) for other in beside_all]


def apply_operator(padded, diag_part, conds):
    center, beside_all = neighbours(padded)
    result = diag_part * center
    for face, other in zip(conds, beside_all):
        result = result + face * (center - other)
    return result


def row_total(diag_part, conds):
    total = diag_part
    for face in conds:
        total = total + face
    return total


def face_gradient(padded_head, padded_adjoint):
    head_c, head_n = neighbours(padded_head)
    adj_c, adj_n = neighbours(padded_adjoint)
    grad = jnp.zeros_like(head_c)
    for head_o, adj_o in zip(head_n, adj_n):
        grad = grad - 0.5 * (adj_c - adj_o) * (head_c - head_o)
    return grad


def rim(state):
    return extended(state)


def on_device(
    head,
    conductivity,
    storage,
    recharge,
    misfit,
    reservoir_cell,
    pumping,
    observed,
    tile_owner,
    tile_inverse,
    zone_of_column,
):
    rows_x, rows_y, layers = head.shape
    count_x = lax.axis_size("gx")
    count_y = lax.axis_size("gy")
    devices = count_x * count_y
    capacity = tile_inverse.shape[0] // devices
    tiles_x = rows_x // AGG
    tiles_y = rows_y // AGG

    def place(values):
        field = jnp.zeros((rows_x * rows_y * layers,), jnp.float32).at[reservoir_cell].add(values)
        return field.reshape(rows_x, rows_y, layers)

    coeff_stack = jnp.stack([conductivity, storage, head])
    padded = extended(coeff_stack)
    conds = conductances(part(padded, 0))
    applied = apply_operator(part(padded, 2), storage, conds)
    total = row_total(storage, conds)
    rhs = jnp.stack([recharge + place(pumping) - applied, misfit + place(observed)])

    def smooth(state):
        for step in range(SWEEPS):
            if state is None:
                state = relax * rhs / total
            else:
                near = extended(state)
                state = state + relax * (rhs - apply_operator(near, storage, conds)) / total
        return state

    owners = tile_owner[:, 0]
    order = jnp.arange(owners.shape[0], dtype=jnp.int32)
    same = owners[:, None] == owners[None, :]
    earlier = order[:, None] > order[None, :]
    rank = jnp.sum(same & earlier, axis=1)
    slot = owners * capacity + rank
    state = None
    for cycle in range(CYCLES):
        state = smooth(state)
        sums = (
            (rhs - apply_operator(rim(state), storage, conds))
            .reshape(2, tiles_x, AGG, tiles_y, AGG, layers)
            .sum(axis=(2, 4))
        )
        tile_rows = (
            jnp.transpose(sums, (1, 2, 0, 3))
            .reshape(tiles_x * tiles_y, 2, layers)
            .astype(jnp.bfloat16)
        )
        outgoing = jnp.zeros((devices * capacity, 2, layers), jnp.bfloat16).at[slot].set(tile_rows)
        product = jnp.einsum(
            "smij,smfj->smfi",
            tile_inverse.reshape(devices, capacity, layers, layers),
            lax.all_to_all(
                outgoing.reshape(devices, capacity, 2, layers),
                ("gx", "gy"),
                split_axis=0,
                concat_axis=0,
                tiled=True,
            ),
            preferred_element_type=jnp.float32,
        )
        returned = lax.all_to_all(product, ("gx", "gy"), split_axis=0, concat_axis=0, tiled=True)
        own_rows = returned.reshape(devices * capacity, 2, layers)[slot]
        spread = jnp.transpose(own_rows.reshape(tiles_x, tiles_y, 2, layers), (2, 0, 1, 3))
        state = state + jnp.repeat(jnp.repeat(spread, AGG, axis=1), AGG, axis=2)
        state = smooth(state)
    new_head = head + state[0]
    final_rim = rim(jnp.stack([new_head, state[1]]))
    grad = face_gradient(part(final_rim, 0), part(final_rim, 1))
    column = jnp.sum(grad, axis=-1) / layers
    zone_total = devices * ZONES_DEV
    local_zones = jax.ops.segment_sum(
        column.reshape(-1), zone_of_column.reshape(-1), num_segments=zone_total
    )
    parts = lax.all_to_all(
        local_zones.reshape(devices, ZONES_DEV), ("gx", "gy"), split_axis=0, concat_axis=0, tiled=True
    )
    zone_gradient = jnp.sum(parts, axis=0)
    return (new_head, zone_gradient)


def solution(mesh):
    placed = (
        P("gx", "gy", None),
        P("gx", "gy", None),
        P("gx", "gy", None),
        P("gx", "gy", None),
        P("gx", "gy", None),
        P(("gx", "gy")),
        P(("gx", "gy")),
        P(("gx", "gy")),
        P(("gx", "gy"), None),
        P(("gx", "gy"), None, None),
        P("gx", "gy"),
    )
    return jax.shard_map(
        on_device,
        mesh=mesh,
        in_specs=placed,
        out_specs=(P("gx", "gy", None), P(("gx", "gy"))),
        check_vma=False,
    )
```

```python
import functools

import jax
import jax.numpy as jnp
from jax import lax
from jax.experimental import pallas as pl
from jax.experimental.pallas import tpu as pltpu
from jax.sharding import PartitionSpec as P

CX, CY, CZ = 32, 48, 128
T = 4
ROWS = CY * 8
PAD = ROWS + 16
TILES = 96
ZDEV = 384
CYCLES = 2
EXCHANGES = 10
RELAX = 0.8
F32, BF16 = jnp.float32, jnp.bfloat16
MESH = pl.DeviceIdType.MESH
CONTRACT_LAST = (((1,), (1,)), ((), ()))


def kernel(
    nx, ny,
    head, cond, stor, rech, misf, cells, pump, obs, owner, mats_in, zone,
    out_head, out_zone,
    nat, mats, kl, hl, kx, hdx, ecf, dg, rs, xs, sx, hx, grad, onat, owner_row, p_out, p_in, zone_hot,
    rbuf, gbuf, cbuf, send_a, recv_a, send_b, recv_b, lz, send_z, recv_z,
    load_sem, mats_sem, out_sem, init_s, init_r, halo_s, halo_r, a_s, a_r, b_s, b_r, z_s, z_r,
):
    n = nx * ny
    me_x, me_y = lax.axis_index("gx"), lax.axis_index("gy")
    me = me_x * ny + me_y
    east, west = (lax.rem(me_x + 1, nx), me_y), (lax.rem(me_x + nx - 1, nx), me_y)
    north, south = (me_x, lax.rem(me_y + 1, ny)), (me_x, lax.rem(me_y + ny - 1, ny))
    in_w, in_e = jnp.where(me_x == 0, 0.0, 1.0), jnp.where(me_x == nx - 1, 0.0, 1.0)
    in_s, in_n = jnp.where(me_y == 0, 0.0, 1.0), jnp.where(me_y == ny - 1, 0.0, 1.0)

    def peer(i):
        other = lax.rem(me + i, n)
        return other, (lax.div(other, ny), lax.rem(other, ny))

    loads = [pltpu.make_async_copy(src, nat.at[i], load_sem.at[i]) for i, src in enumerate((cond, head, stor, rech, misf))]
    for copy in loads:
        copy.start()
    mats_copy = pltpu.make_async_copy(mats_in, mats, mats_sem)
    mats_copy.start()

    barrier = pltpu.get_barrier_semaphore()

    def greet(i, carry):
        pl.semaphore_signal(barrier, inc=1, device_id=peer(i)[1], device_id_type=MESH)
        return carry

    lax.fori_loop(1, n, greet, 0)

    def relayout(i, dst, offset):
        def one(t, carry):
            for s in range(8):
                for block in range(CY // 8):
                    dst[t, pl.ds(offset + block * 64 + s, 8, stride=8), :] = nat[i, 4 * s + t, block * 8:block * 8 + 8, :]
            return carry

        lax.fori_loop(0, T, one, 0)

    loads[0].wait()
    relayout(0, kl, 8)
    loads[1].wait()
    relayout(1, hl, 8)

    pl.semaphore_wait(barrier, n - 1)

    def remote(src, dst, send, recv, device):
        copy = pltpu.make_async_remote_copy(src, dst, send, recv, device_id=device, device_id_type=MESH)
        copy.start()
        return copy

    first = []
    for i, (lay, side) in enumerate(((kl, kx), (hl, hdx))):
        first += [
            remote(nat.at[i, CX - 1], side.at[0], init_s.at[4 * i], init_r.at[4 * i], east),
            remote(nat.at[i, 0], side.at[1], init_s.at[4 * i + 1], init_r.at[4 * i + 1], west),
            remote(lay.at[:, ROWS:ROWS + 8], lay.at[:, 0:8], init_s.at[4 * i + 2], init_r.at[4 * i + 2], north),
            remote(lay.at[:, 8:16], lay.at[:, ROWS + 8:PAD], init_s.at[4 * i + 3], init_r.at[4 * i + 3], south),
        ]

    loads[2].wait()
    relayout(2, dg, 0)
    loads[3].wait()
    relayout(3, rs.at[0], 0)
    loads[4].wait()
    relayout(4, rs.at[1], 0)

    count = cells.shape[1]
    cell = cells[...]
    column = lax.shift_right_logical(cell, 7)
    cell_z = (cell & 127).astype(F32)
    cell_x = jnp.floor((column.astype(F32) + 0.5) * (1.0 / CY)).astype(jnp.int32)
    cell_row = (cell_x & 3) * ROWS + (column - cell_x * CY) * 8 + lax.shift_right_logical(cell_x, 2)
    diag = lax.broadcasted_iota(jnp.int32, (count, count), 0) == lax.broadcasted_iota(jnp.int32, (count, count), 1)

    def upright(row, mask):
        return jnp.sum(jnp.where(mask, jnp.broadcast_to(row, mask.shape), 0.0), axis=1, keepdims=True)

    at_z = lax.broadcasted_iota(jnp.int32, (count, CZ), 1) == upright(cell_z, diag).astype(jnp.int32)
    values = jnp.concatenate([jnp.where(at_z, upright(v[...], diag), 0.0) for v in (pump, obs)], axis=1)
    value_parts = []
    for _ in range(3):
        value_parts.append(values.astype(BF16))
        values = values - value_parts[-1].astype(F32)

    def put_reservoirs(t, carry):
        rows = lax.broadcasted_iota(jnp.int32, (ROWS, count), 0) + t * ROWS
        hot = jnp.where(rows == cell_row, 1.0, 0.0).astype(BF16)
        field = sum(jnp.dot(hot, part, preferred_element_type=F32) for part in value_parts)
        rs[0, t] += field[:, :CZ]
        rs[1, t] += field[:, CZ:]
        return carry

    lax.fori_loop(0, T, put_reservoirs, 0)

    lane = lax.broadcasted_iota(jnp.int32, (128, 128), 1)
    sub = lax.broadcasted_iota(jnp.int32, (128, 128), 0)
    owner_row[...] = -1000.0 - lane[0:1].astype(F32)
    owner_row[0:1, 0:TILES] = owner[...].astype(F32)
    orow = owner_row[...]
    ocol = upright(orow, lane == sub)
    same = ocol == orow
    rank_row = jnp.sum(jnp.where(same & (sub < lane), 1.0, 0.0), axis=0, keepdims=True)
    rank_col = jnp.sum(jnp.where(same & (lane < sub), 1.0, 0.0), axis=1, keepdims=True)
    code_row = orow * 4.0 + rank_row * 2.0
    code_col = ocol * 4.0 + rank_col * 2.0
    down = lax.broadcasted_iota(jnp.int32, (4 * n, 128), 0).astype(F32)
    across = lax.broadcasted_iota(jnp.int32, (128, 4 * n), 1).astype(F32)
    for f in range(2):
        p_out[:, f * 128:f * 128 + 128] = jnp.where(down == code_row + float(f), 1.0, 0.0).astype(BF16)
        p_in[f * 128:f * 128 + 128, :] = jnp.where(across == code_col + float(f), 1.0, 0.0).astype(BF16)
    rbuf[...] = jnp.zeros_like(rbuf)

    zones = zone[...].astype(F32)
    zone_dev = jnp.floor((zones + 0.5) * (1.0 / ZDEV))
    zone_local = zones - zone_dev * ZDEV
    for block in range(T):
        cut = slice(block * ROWS, block * ROWS + ROWS)
        rows = lax.broadcasted_iota(jnp.int32, (ZDEV, ROWS), 0).astype(F32)
        zone_hot[:, cut] = jnp.where(rows == zone_local[:, cut], 1.0, 0.0).astype(BF16)

    for copy in first:
        copy.wait()
    for lay in (kl, hl):
        lay[:, 0:8] = lay[:, 0:8] * in_s
        lay[:, ROWS + 8:PAD] = lay[:, ROWS + 8:PAD] * in_n
    for side in (kx, hdx):
        side[0] = side[0] * in_w
        side[1] = side[1] * in_e

    sub8 = lax.broadcasted_iota(jnp.int32, (8, CZ), 0)
    lane8 = lax.broadcasted_iota(jnp.int32, (8, CZ), 1)
    low_s, high_s, low_z, high_z = sub8 == 0, sub8 == 7, lane8 == 0, lane8 == CZ - 1

    def beside(tile, west_row, east_row, t, y, wrap_z):
        row = pl.multiple_of(y * 8, 8)
        center = tile(t, row + 8)
        if t == 0:
            wst = jnp.where(low_s, jnp.broadcast_to(west_row(y), (8, CZ)), pltpu.roll(tile(T - 1, row + 8), 1, 0))
        else:
            wst = tile(t - 1, row + 8)
        if t == T - 1:
            est = jnp.where(high_s, jnp.broadcast_to(east_row(y), (8, CZ)), pltpu.roll(tile(0, row + 8), 7, 0))
        else:
            est = tile(t + 1, row + 8)
        below, above = pltpu.roll(center, 1, 1), pltpu.roll(center, CZ - 1, 1)
        if not wrap_z:
            below, above = jnp.where(low_z, 0.0, below), jnp.where(high_z, 0.0, above)
        return center, (wst, est, tile(t, row), tile(t, row + 16), below, above)

    def plain(ref):
        return lambda t, row: ref[t, pl.ds(pl.multiple_of(row, 8), 8), :]

    def field_of(p, f):
        return lambda t, row: xs[p, f, t, pl.ds(pl.multiple_of(row, 8), 8), :]

    def side_row(ref, side):
        return lambda y: ref[side, pl.ds(y, 1), :]

    def halo_row(k, side, f):
        return lambda y: hx[k, side, f, pl.ds(y, 1), :]

    def put(p, k, f, t, y, value):
        xs[p, f, t, pl.ds(pl.multiple_of(y * 8 + 8, 8), 8), :] = value
        if t == 0:
            sx[k, 0, f, pl.ds(y, 1), :] = value[0:1]
        if t == T - 1:
            sx[k, 1, f, pl.ds(y, 1), :] = value[7:8]

    def exchange(p, k):
        return [
            remote(sx.at[k, 1], hx.at[k, 0], halo_s.at[k, 0], halo_r.at[k, 0], east),
            remote(sx.at[k, 0], hx.at[k, 1], halo_s.at[k, 1], halo_r.at[k, 1], west),
            remote(xs.at[p, :, :, ROWS:ROWS + 8], xs.at[p, :, :, 0:8], halo_s.at[k, 2], halo_r.at[k, 2], north),
            remote(xs.at[p, :, :, 8:16], xs.at[p, :, :, ROWS + 8:PAD], halo_s.at[k, 3], halo_r.at[k, 3], south),
        ]

    def prepare(y, carry):
        row = pl.multiple_of(y * 8, 8)
        for t in range(T):
            here = (t, pl.ds(row, 8), slice(None))
            k_c, k_all = beside(plain(kl), side_row(kx, 0), side_row(kx, 1), t, y, False)
            h_c, h_all = beside(plain(hl), side_row(hdx, 0), side_row(hdx, 1), t, y, False)
            faces = [0.5 * (k_c + other) for other in k_all]
            storage = dg[here]
            total = storage
            applied = storage * h_c
            for face, other in zip(faces, h_all):
                total = total + face
                applied = applied + face * (h_c - other)
            gain = RELAX / total
            dg[here] = total * (1.0 / RELAX)
            faces[0] = faces[0] if t else jnp.where(low_s, faces[0] * in_w, faces[0])
            faces[1] = faces[1] if t < T - 1 else jnp.where(high_s, faces[1] * in_e, faces[1])
            faces[4] = jnp.where(low_z, 0.0, faces[4])
            faces[5] = jnp.where(high_z, 0.0, faces[5])
            for j in range(6):
                ecf[j, t, pl.ds(row, 8), :] = faces[j] * gain
            for f in range(2):
                rhs = rs[f, t, pl.ds(row, 8), :]
                rhs = (rhs - applied if f == 0 else rhs) * gain
                rs[f, t, pl.ds(row, 8), :] = rhs
                put(0, 0, f, t, y, rhs)
        return carry

    lax.fori_loop(0, CY, prepare, 0)
    ecf[2, :, 0:8] = ecf[2, :, 0:8] * in_s
    ecf[3, :, ROWS - 8:ROWS] = ecf[3, :, ROWS - 8:ROWS] * in_n

    def change(p, k, t, y):
        row = pl.multiple_of(y * 8, 8)
        factors = [ecf[j, t, pl.ds(row, 8), :] for j in range(6)]
        result = []
        for f in range(2):
            center, others = beside(field_of(p, f), halo_row(k, 0, f), halo_row(k, 1, f), t, y, True)
            total = rs[f, t, pl.ds(row, 8), :]
            for factor, other in zip(factors, others):
                total = total + factor * other
            result.append((center, total))
        return result

    def sweep(p, k):
        q = 1 - p

        def one(y, carry):
            for t in range(T):
                for f, (center, total) in enumerate(change(p, k, t, y)):
                    put(q, k + 1, f, t, y, (1.0 - RELAX) * center + total)
            return carry

        lax.fori_loop(0, CY, one, 0)

    def residual(p, k):
        def one(b, carry):
            sums = [jnp.zeros((8, CZ), F32) for _ in range(2)]
            for j in range(4):
                y = b * 4 + j
                for t in range(T):
                    scale = dg[t, pl.ds(pl.multiple_of(y * 8, 8), 8), :]
                    for f, (center, total) in enumerate(change(p, k, t, y)):
                        sums[f] = sums[f] + scale * (total - RELAX * center)
            for f in range(2):
                rbuf[pl.ds(f * 128 + b, 8, stride=12), :] = sums[f]
            return carry

        lax.fori_loop(0, CY // 4, one, 0)

    def all_to_all(src, dst, send, recv, own):
        keep = pltpu.make_async_copy(src.at[me], dst.at[me], recv)
        keep.start()

        def one(i, carry):
            other, device = peer(i)
            pltpu.make_async_remote_copy(
                src.at[other], dst.at[me], send, recv, device_id=device, device_id_type=MESH
            ).start()
            return carry

        lax.fori_loop(1, n, one, 0)

    def finish(src, dst, send, recv):
        pltpu.make_async_copy(dst, dst, recv).wait()
        pltpu.make_async_copy(src.at[0:n - 1], src.at[0:n - 1], send).wait()

    def coarse(cycle):
        gbuf[...] = jnp.dot(p_out[...], rbuf[...].astype(BF16), preferred_element_type=F32)

        def pack(i, carry):
            rows = gbuf[pl.ds(pl.multiple_of(i * 8, 8), 8), :].astype(BF16)
            send_a[cycle, 2 * i] = rows[0:4]
            send_a[cycle, 2 * i + 1] = rows[4:8]
            return carry

        lax.fori_loop(0, n // 2, pack, 0, unroll=4)
        all_to_all(send_a.at[cycle], recv_a.at[cycle], a_s.at[cycle], a_r.at[cycle], me)
        if cycle == 0:
            mats_copy.wait()
        finish(send_a.at[cycle], recv_a.at[cycle], a_s.at[cycle], a_r.at[cycle])
        first_slot = lax.broadcasted_iota(jnp.int32, (4, CZ), 0) < 2

        def apply(i, carry):
            both = mats[pl.ds(2 * i, 2)].reshape(2 * CZ, CZ)
            product = lax.dot_general(recv_a[cycle, i], both, CONTRACT_LAST, preferred_element_type=F32)
            send_b[cycle, i] = jnp.where(first_slot, product[:, :CZ], product[:, CZ:])
            return carry

        lax.fori_loop(0, n, apply, 0, unroll=8)
        all_to_all(send_b.at[cycle], recv_b.at[cycle], b_s.at[cycle], b_r.at[cycle], me)
        finish(send_b.at[cycle], recv_b.at[cycle], b_s.at[cycle], b_r.at[cycle])

        def unpack(i, carry):
            gbuf[pl.ds(pl.multiple_of(i * 8, 8), 8), :] = jnp.concatenate(
                [recv_b[cycle, 2 * i], recv_b[cycle, 2 * i + 1]], axis=0
            )
            return carry

        lax.fori_loop(0, n // 2, unpack, 0, unroll=4)
        rows = gbuf[...]
        high = rows.astype(BF16)
        low = (rows - high.astype(F32)).astype(BF16)
        cbuf[...] = jnp.dot(p_in[...], high, preferred_element_type=F32) + jnp.dot(
            p_in[...], low, preferred_element_type=F32
        )

    def correct(p, k):
        q = 1 - p

        def one(b, carry):
            for f in range(2):
                extra = cbuf[pl.ds(f * 128 + b, 8, stride=12), :]
                for j in range(4):
                    y = b * 4 + j
                    for t in range(T):
                        put(q, k, f, t, y, field_of(p, f)(t, y * 8 + 8) + extra)
            return carry

        lax.fori_loop(0, CY // 4, one, 0)

    def arrive(copies):
        for copy in copies:
            copy.wait()

    k, p = 0, 0
    moving = exchange(p, k)
    for cycle in range(CYCLES):
        for step in range(1 if cycle == 0 else 2):
            arrive(moving)
            sweep(p, k)
            k, p = k + 1, 1 - p
            moving = exchange(p, k)
        arrive(moving)
        residual(p, k)
        coarse(cycle)
        k = k + 1
        correct(p, k)
        p = 1 - p
        moving = exchange(p, k)
        for step in range(2):
            arrive(moving)
            sweep(p, k)
            k, p = k + 1, 1 - p
            moving = exchange(p, k)

    arrive(moving)
    for f in range(2):
        xs[p, f, :, 0:8] = xs[p, f, :, 0:8] * in_s
        xs[p, f, :, ROWS + 8:PAD] = xs[p, f, :, ROWS + 8:PAD] * in_n
        hx[k, 0, f] = hx[k, 0, f] * in_w
        hx[k, 1, f] = hx[k, 1, f] * in_e
    for side in range(2):
        hdx[side] = hdx[side] + hx[k, side, 0]

    def update(i, carry):
        row = pl.multiple_of(i * 8, 8)
        for t in range(T):
            hl[t, pl.ds(row, 8), :] = hl[t, pl.ds(row, 8), :] + xs[p, 0, t, pl.ds(row, 8), :]
        return carry

    lax.fori_loop(0, PAD // 8, update, 0)

    def gradient(y, carry):
        for t in range(T):
            h_c, h_all = beside(plain(hl), side_row(hdx, 0), side_row(hdx, 1), t, y, False)
            a_c, a_all = beside(field_of(p, 1), halo_row(k, 0, 1), halo_row(k, 1, 1), t, y, False)
            total = jnp.zeros((8, CZ), F32)
            for h_o, a_o in zip(h_all, a_all):
                total = total + (a_c - a_o) * (h_c - h_o)
            grad[pl.ds(pl.multiple_of(t * ROWS + y * 8, 8), 8), :] = total
        return carry

    lax.fori_loop(0, CY, gradient, 0)

    ones = jnp.ones((8, CZ), BF16)
    for block in range(T):
        cut = slice(block * ROWS, block * ROWS + ROWS)
        rows = grad[cut, :]
        high = rows.astype(BF16)
        low = (rows - high.astype(F32)).astype(BF16)
        column = lax.dot_general(ones, high, CONTRACT_LAST, preferred_element_type=F32)
        column = column + lax.dot_general(ones, low, CONTRACT_LAST, preferred_element_type=F32)
        column = column[0:1] * (-0.5 / CZ)
        high = column.astype(BF16).astype(F32)
        low = column - high
        mine = lax.broadcasted_iota(jnp.int32, (n, ROWS), 0).astype(F32) == zone_dev[:, cut]
        parts = jnp.zeros((n, ZDEV), F32)
        for value in (high, low):
            spread = jnp.where(mine, value, 0.0).astype(BF16)
            parts = parts + lax.dot_general(spread, zone_hot[:, cut], CONTRACT_LAST, preferred_element_type=F32)
        if block == 0:
            lz[...] = parts
        else:
            lz[...] += parts

    def pack_zones(i, carry):
        rows = lz[pl.ds(pl.multiple_of(i * 8, 8), 8), :]
        for j in range(8):
            send_z[8 * i + j] = rows[j:j + 1]
        return carry

    lax.fori_loop(0, n // 8, pack_zones, 0)
    all_to_all(send_z, recv_z, z_s, z_r, me)

    def natural(t, carry):
        for s in range(8):
            for block in range(CY // 8):
                onat[4 * s + t, block * 8:block * 8 + 8, :] = hl[t, pl.ds(8 + block * 64 + s, 8, stride=8), :]
        return carry

    lax.fori_loop(0, T, natural, 0)
    out_copy = pltpu.make_async_copy(onat, out_head, out_sem)
    out_copy.start()
    finish(send_z, recv_z, z_s, z_r)

    def add_zones(i, total):
        return total + recv_z[i]

    out_zone[...] = lax.fori_loop(0, n, add_zones, jnp.zeros((1, ZDEV), F32), unroll=8)
    out_copy.wait()


def on_device(
    head, conductivity, storage, recharge, misfit, reservoir_cell, pumping, observed, tile_owner, tile_inverse, zone_of_column
):
    nx, ny = lax.axis_size("gx"), lax.axis_size("gy")
    n = nx * ny
    zone = jnp.transpose(zone_of_column.reshape(8, T, CY), (1, 2, 0)).reshape(1, CX * CY)
    anywhere, vmem = pl.BlockSpec(memory_space=pl.ANY), pl.BlockSpec(memory_space=pltpu.VMEM)
    dma = pltpu.SemaphoreType.DMA
    new_head, zones = pl.pallas_call(
        functools.partial(kernel, nx, ny),
        out_shape=(
            jax.ShapeDtypeStruct((CX, CY, CZ), F32),
            jax.ShapeDtypeStruct((1, ZDEV), F32),
        ),
        in_specs=[anywhere] * 5 + [vmem] * 4 + [anywhere, vmem],
        out_specs=(anywhere, vmem),
        scratch_shapes=[
            pltpu.VMEM((5, CX, CY, CZ), F32),
            pltpu.VMEM((2 * n, CZ, CZ), BF16),
            pltpu.VMEM((T, PAD, CZ), F32),
            pltpu.VMEM((T, PAD, CZ), F32),
            pltpu.VMEM((2, CY, CZ), F32),
            pltpu.VMEM((2, CY, CZ), F32),
            pltpu.VMEM((6, T, ROWS, CZ), F32),
            pltpu.VMEM((T, ROWS, CZ), F32),
            pltpu.VMEM((2, T, ROWS, CZ), F32),
            pltpu.VMEM((2, 2, T, PAD, CZ), F32),
            pltpu.VMEM((EXCHANGES, 2, 2, CY, CZ), F32),
            pltpu.VMEM((EXCHANGES, 2, 2, CY, CZ), F32),
            pltpu.VMEM((CX * CY, CZ), F32),
            pltpu.VMEM((CX, CY, CZ), F32),
            pltpu.VMEM((1, 128), F32),
            pltpu.VMEM((4 * n, 256), BF16),
            pltpu.VMEM((256, 4 * n), BF16),
            pltpu.VMEM((ZDEV, CX * CY), BF16),
            pltpu.VMEM((256, CZ), F32),
            pltpu.VMEM((4 * n, CZ), F32),
            pltpu.VMEM((256, CZ), F32),
            pltpu.VMEM((CYCLES, n, 4, CZ), BF16),
            pltpu.VMEM((CYCLES, n, 4, CZ), BF16),
            pltpu.VMEM((CYCLES, n, 4, CZ), F32),
            pltpu.VMEM((CYCLES, n, 4, CZ), F32),
            pltpu.VMEM((n, ZDEV), F32),
            pltpu.VMEM((n, 1, ZDEV), F32),
            pltpu.VMEM((n, 1, ZDEV), F32),
            dma((5,)), dma, dma, dma((8,)), dma((8,)), dma((EXCHANGES, 4)), dma((EXCHANGES, 4)),
            dma((CYCLES,)), dma((CYCLES,)), dma((CYCLES,)), dma((CYCLES,)), dma, dma,
        ],
        compiler_params=pltpu.CompilerParams(
            collective_id=0, has_side_effects=True, vmem_limit_bytes=60 * 1024 * 1024
        ),
        name="newton",
    )(
        head, conductivity, storage, recharge, misfit, reservoir_cell.reshape(1, -1), pumping.reshape(1, -1),
        observed.reshape(1, -1), tile_owner.reshape(1, -1), tile_inverse, zone,
    )
    return new_head, zones.reshape(ZDEV)


def solution(mesh):
    block, flat = P("gx", "gy", None), P(("gx", "gy"))
    placed = (block,) * 5 + (flat,) * 3 + (P(("gx", "gy"), None), P(("gx", "gy"), None, None), P("gx", "gy"))
    return jax.shard_map(
        on_device, mesh=mesh, in_specs=placed, out_specs=(block, flat), check_vma=False
    )
```

```python
import functools

import jax
import jax.numpy as jnp
from jax import lax
from jax.experimental import pallas as pl
from jax.experimental.pallas import tpu as pltpu
from jax.sharding import PartitionSpec as P

CX, CY, CZ = 32, 48, 128
T = 4
ROWS = CY * 8
PAD = ROWS + 16
TILES = 96
ZDEV = 384
CYCLES = 2
EXCHANGES = 10
RELAX = 0.8
F32, BF16 = jnp.float32, jnp.bfloat16
MESH = pl.DeviceIdType.MESH
CONTRACT_LAST = (((1,), (1,)), ((), ()))


def kernel(
    nx, ny,
    head, cond, stor, rech, misf, cells, pump, obs, owner, mats_in, zone,
    out_head, out_zone,
    nat, mats, kl, hl, kx, hdx, ecf, dg, rs, xa, xb, sx, hx, edge_x, face_x, edge_y, face_y, prods, grad, onat, owner_row, p_out, p_in, zone_hot,
    rbuf, gbuf, cbuf, send_a, recv_a, send_b, recv_b, lz, send_z, recv_z,
    load_sem, mats_sem, out_sem, init_s, init_r, halo_s, halo_r, a_s, a_r, b_s, b_r, z_s, z_r,
):
    n = nx * ny
    xs = (xa, xb)
    me_x, me_y = lax.axis_index("gx"), lax.axis_index("gy")
    me = me_x * ny + me_y
    east, west = (lax.rem(me_x + 1, nx), me_y), (lax.rem(me_x + nx - 1, nx), me_y)
    north, south = (me_x, lax.rem(me_y + 1, ny)), (me_x, lax.rem(me_y + ny - 1, ny))
    in_w, in_e = jnp.where(me_x == 0, 0.0, 1.0), jnp.where(me_x == nx - 1, 0.0, 1.0)
    in_s, in_n = jnp.where(me_y == 0, 0.0, 1.0), jnp.where(me_y == ny - 1, 0.0, 1.0)

    def peer(i):
        other = lax.rem(me + i, n)
        return other, (lax.div(other, ny), lax.rem(other, ny))

    loads = [pltpu.make_async_copy(src, nat.at[i], load_sem.at[i]) for i, src in enumerate((cond, head, stor, rech, misf))]
    for copy in loads:
        copy.start()
    mats_copy = pltpu.make_async_copy(mats_in, mats, mats_sem)
    mats_copy.start()

    barrier = pltpu.get_barrier_semaphore()

    def greet(i, carry):
        pl.semaphore_signal(barrier, inc=1, device_id=peer(i)[1], device_id_type=MESH)
        return carry

    lax.fori_loop(1, n, greet, 0)

    def relayout(i, dst, offset):
        def one(t, carry):
            for s in range(8):
                for block in range(CY // 8):
                    dst[t, pl.ds(offset + block * 64 + s, 8, stride=8), :] = nat[i, 4 * s + t, block * 8:block * 8 + 8, :]
            return carry

        lax.fori_loop(0, T, one, 0)

    loads[0].wait()
    relayout(0, kl, 8)
    loads[1].wait()
    relayout(1, hl, 8)

    pl.semaphore_wait(barrier, n - 1)

    def remote(src, dst, send, recv, device):
        copy = pltpu.make_async_remote_copy(src, dst, send, recv, device_id=device, device_id_type=MESH)
        copy.start()
        return copy

    first = []
    for i, (lay, side) in enumerate(((kl, kx), (hl, hdx))):
        first += [
            remote(nat.at[i, CX - 1], side.at[0], init_s.at[4 * i], init_r.at[4 * i], east),
            remote(nat.at[i, 0], side.at[1], init_s.at[4 * i + 1], init_r.at[4 * i + 1], west),
            remote(lay.at[:, ROWS:ROWS + 8], lay.at[:, 0:8], init_s.at[4 * i + 2], init_r.at[4 * i + 2], north),
            remote(lay.at[:, 8:16], lay.at[:, ROWS + 8:PAD], init_s.at[4 * i + 3], init_r.at[4 * i + 3], south),
        ]

    loads[2].wait()
    relayout(2, dg, 0)
    loads[3].wait()
    relayout(3, rs.at[0], 0)
    loads[4].wait()
    relayout(4, rs.at[1], 0)

    count = cells.shape[1]
    cell = cells[...]
    column = lax.shift_right_logical(cell, 7)
    cell_z = (cell & 127).astype(F32)
    cell_x = jnp.floor((column.astype(F32) + 0.5) * (1.0 / CY)).astype(jnp.int32)
    cell_row = (cell_x & 3) * ROWS + (column - cell_x * CY) * 8 + lax.shift_right_logical(cell_x, 2)
    diag = lax.broadcasted_iota(jnp.int32, (count, count), 0) == lax.broadcasted_iota(jnp.int32, (count, count), 1)

    def upright(row, mask):
        return jnp.sum(jnp.where(mask, jnp.broadcast_to(row, mask.shape), 0.0), axis=1, keepdims=True)

    at_z = lax.broadcasted_iota(jnp.int32, (count, CZ), 1) == upright(cell_z, diag).astype(jnp.int32)
    values = jnp.concatenate([jnp.where(at_z, upright(v[...], diag), 0.0) for v in (pump, obs)], axis=1)
    value_parts = []
    for _ in range(3):
        value_parts.append(values.astype(BF16))
        values = values - value_parts[-1].astype(F32)

    def put_reservoirs(t, carry):
        rows = lax.broadcasted_iota(jnp.int32, (ROWS, count), 0) + t * ROWS
        hot = jnp.where(rows == cell_row, 1.0, 0.0).astype(BF16)
        field = sum(jnp.dot(hot, part, preferred_element_type=F32) for part in value_parts)
        rs[0, t] += field[:, :CZ]
        rs[1, t] += field[:, CZ:]
        return carry

    lax.fori_loop(0, T, put_reservoirs, 0)

    lane = lax.broadcasted_iota(jnp.int32, (128, 128), 1)
    sub = lax.broadcasted_iota(jnp.int32, (128, 128), 0)
    owner_row[...] = -1000.0 - lane[0:1].astype(F32)
    owner_row[0:1, 0:TILES] = owner[...].astype(F32)
    orow = owner_row[...]
    ocol = upright(orow, lane == sub)
    same = ocol == orow
    rank_row = jnp.sum(jnp.where(same & (sub < lane), 1.0, 0.0), axis=0, keepdims=True)
    rank_col = jnp.sum(jnp.where(same & (lane < sub), 1.0, 0.0), axis=1, keepdims=True)
    code_row = orow * 4.0 + rank_row * 2.0
    code_col = ocol * 4.0 + rank_col * 2.0
    down = lax.broadcasted_iota(jnp.int32, (4 * n, 128), 0).astype(F32)
    across = lax.broadcasted_iota(jnp.int32, (128, 4 * n), 1).astype(F32)
    for f in range(2):
        p_out[:, f * 128:f * 128 + 128] = jnp.where(down == code_row + float(f), 1.0, 0.0).astype(BF16)
        p_in[f * 128:f * 128 + 128, :] = jnp.where(across == code_col + float(f), 1.0, 0.0).astype(BF16)
    rbuf[...] = jnp.zeros_like(rbuf)

    zones = zone[...].astype(F32)
    zone_dev = jnp.floor((zones + 0.5) * (1.0 / ZDEV))
    zone_local = zones - zone_dev * ZDEV
    for block in range(T):
        cut = slice(block * ROWS, block * ROWS + ROWS)
        rows = lax.broadcasted_iota(jnp.int32, (ZDEV, ROWS), 0).astype(F32)
        zone_hot[:, cut] = jnp.where(rows == zone_local[:, cut], 1.0, 0.0).astype(BF16)

    for copy in first:
        copy.wait()
    for lay in (kl, hl):
        lay[:, 0:8] = lay[:, 0:8] * in_s
        lay[:, ROWS + 8:PAD] = lay[:, ROWS + 8:PAD] * in_n
    for side in (kx, hdx):
        side[0] = side[0] * in_w
        side[1] = side[1] * in_e

    sub8 = lax.broadcasted_iota(jnp.int32, (8, CZ), 0)
    lane8 = lax.broadcasted_iota(jnp.int32, (8, CZ), 1)
    low_s, high_s, low_z, high_z = sub8 == 0, sub8 == 7, lane8 == 0, lane8 == CZ - 1

    def beside(tile, west_row, east_row, t, y, wrap_z):
        row = pl.multiple_of(y * 8, 8)
        center = tile(t, row + 8)
        if t == 0:
            wst = jnp.where(low_s, jnp.broadcast_to(west_row(y), (8, CZ)), pltpu.roll(tile(T - 1, row + 8), 1, 0))
        else:
            wst = tile(t - 1, row + 8)
        if t == T - 1:
            est = jnp.where(high_s, jnp.broadcast_to(east_row(y), (8, CZ)), pltpu.roll(tile(0, row + 8), 7, 0))
        else:
            est = tile(t + 1, row + 8)
        below, above = pltpu.roll(center, 1, 1), pltpu.roll(center, CZ - 1, 1)
        if not wrap_z:
            below, above = jnp.where(low_z, 0.0, below), jnp.where(high_z, 0.0, above)
        return center, (wst, est, tile(t, row), tile(t, row + 16), below, above)

    def plain(ref):
        return lambda t, row: ref[t, pl.ds(pl.multiple_of(row, 8), 8), :]

    def field_of(p, f):
        return lambda t, row: xs[p][f, t, pl.ds(pl.multiple_of(row, 8), 8), :]

    def side_row(ref, side):
        return lambda y: ref[side, pl.ds(y, 1), :]

    def halo_row(k, side, f):
        return lambda y: hx[k, side, f, pl.ds(y, 1), :]

    def put(p, k, f, t, y, value):
        xs[p][f, t, pl.ds(pl.multiple_of(y * 8 + 8, 8), 8), :] = value
        if t == 0:
            sx[k, 0, f, pl.ds(y, 1), :] = value[0:1]
        if t == T - 1:
            sx[k, 1, f, pl.ds(y, 1), :] = value[7:8]

    def exchange(p, k):
        return [
            remote(sx.at[k, 1], hx.at[k, 0], halo_s.at[k, 0], halo_r.at[k, 0], east),
            remote(sx.at[k, 0], hx.at[k, 1], halo_s.at[k, 1], halo_r.at[k, 1], west),
            remote(xs[p].at[:, :, ROWS:ROWS + 8], xs[p].at[:, :, 0:8], halo_s.at[k, 2], halo_r.at[k, 2], north),
            remote(xs[p].at[:, :, 8:16], xs[p].at[:, :, ROWS + 8:PAD], halo_s.at[k, 3], halo_r.at[k, 3], south),
        ]

    def prepare(y, carry):
        row = pl.multiple_of(y * 8, 8)
        for t in range(T):
            here = (t, pl.ds(row, 8), slice(None))
            k_c, k_all = beside(plain(kl), side_row(kx, 0), side_row(kx, 1), t, y, False)
            h_c, h_all = beside(plain(hl), side_row(hdx, 0), side_row(hdx, 1), t, y, False)
            faces = [0.5 * (k_c + other) for other in k_all]
            storage = dg[here]
            total = storage
            applied = storage * h_c
            for face, other in zip(faces, h_all):
                total = total + face
                applied = applied + face * (h_c - other)
            gain = RELAX / total
            dg[here] = total * (1.0 / RELAX)
            faces[0] = faces[0] if t else jnp.where(low_s, faces[0] * in_w, faces[0])
            faces[1] = faces[1] if t < T - 1 else jnp.where(high_s, faces[1] * in_e, faces[1])
            faces[4] = jnp.where(low_z, 0.0, faces[4])
            faces[5] = jnp.where(high_z, 0.0, faces[5])
            for j in range(6):
                ecf[j, t, pl.ds(row, 8), :] = faces[j] * gain
            for f in range(2):
                rhs = rs[f, t, pl.ds(row, 8), :]
                rhs = (rhs - applied if f == 0 else rhs) * gain
                rs[f, t, pl.ds(row, 8), :] = rhs
                put(0, 0, f, t, y, rhs)
        return carry

    lax.fori_loop(0, CY, prepare, 0, unroll=2)

    def split_edges():
        edge_y[0] = ecf[2, :, 0:8] * in_s
        edge_y[1] = ecf[3, :, ROWS - 8:ROWS] * in_n
        face_y[0] = edge_y[0] * dg[:, 0:8]
        face_y[1] = edge_y[1] * dg[:, ROWS - 8:ROWS]
        for block in range(CY // 8):
            cut = slice(block * 8, block * 8 + 8)
            for side, t, s in ((0, 0, 0), (1, T - 1, 7)):
                rows = pl.ds(block * 64 + s, 8, stride=8)
                edge_x[side, cut] = ecf[side, t, rows, :]
                face_x[side, cut] = edge_x[side, cut] * dg[t, rows, :]

        def clear(y, carry):
            rows = pl.ds(pl.multiple_of(y * 8, 8), 8)
            ecf[0, 0, rows, :] = jnp.where(low_s, 0.0, ecf[0, 0, rows, :])
            ecf[1, T - 1, rows, :] = jnp.where(high_s, 0.0, ecf[1, T - 1, rows, :])
            return carry

        lax.fori_loop(0, CY, clear, 0, unroll=8)

    def change(p, t, y, south=True, north=True):
        row = pl.multiple_of(y * 8, 8)
        factors = [ecf[j, t, pl.ds(row, 8), :] for j in range(6)]
        result = []
        for f in range(2):
            tile = field_of(p, f)
            center = tile(t, row + 8)
            wst = tile(t - 1, row + 8) if t else pltpu.roll(tile(T - 1, row + 8), 1, 0)
            est = tile(t + 1, row + 8) if t < T - 1 else pltpu.roll(tile(0, row + 8), 7, 0)
            others = [wst, est, tile(t, row) if south else None, tile(t, row + 16) if north else None]
            others += [pltpu.roll(center, 1, 1), pltpu.roll(center, CZ - 1, 1)]
            total = rs[f, t, pl.ds(row, 8), :]
            for factor, other in zip(factors, others):
                if other is not None:
                    total = total + factor * other
            result.append((center, total))
        return result

    def sweep(p):
        q = 1 - p

        def row_of(y, **sides):
            for t in range(T):
                for f, (center, total) in enumerate(change(p, t, y, **sides)):
                    xs[q][f, t, pl.ds(pl.multiple_of(y * 8 + 8, 8), 8), :] = (1.0 - RELAX) * center + total

        def one(i, carry):
            row_of(2 * i + 1)
            row_of(2 * i + 2)
            return carry

        row_of(0, south=False)
        lax.fori_loop(0, CY // 2 - 1, one, 0)
        row_of(CY - 1, north=False)

    def sweep_edges(p, k):
        q = 1 - p
        for f in range(2):
            for t in range(T):
                xs[q][f, t, 8:16] += edge_y[0, t] * xs[p][f, t, 0:8]
                xs[q][f, t, ROWS:ROWS + 8] += edge_y[1, t] * xs[p][f, t, ROWS + 8:PAD]
            for block in range(CY // 8):
                cut = slice(block * 8, block * 8 + 8)
                for side, t, s in ((0, 0, 0), (1, T - 1, 7)):
                    rows = pl.ds(8 + block * 64 + s, 8, stride=8)
                    value = xs[q][f, t, rows, :] + edge_x[side, cut] * hx[k, side, f, cut]
                    xs[q][f, t, rows, :] = value
                    sx[k + 1, side, f, cut] = value

    def residual(p):
        def block_of(b, first=False, last=False):
            sums = [jnp.zeros((8, CZ), F32) for _ in range(2)]
            for j in range(4):
                y = b * 4 + j
                for t in range(T):
                    scale = dg[t, pl.ds(pl.multiple_of(y * 8, 8), 8), :]
                    both = change(p, t, y, south=not (first and j == 0), north=not (last and j == 3))
                    for f, (center, total) in enumerate(both):
                        sums[f] = sums[f] + scale * (total - RELAX * center)
            for f in range(2):
                rbuf[pl.ds(f * 128 + b, 8, stride=12), :] = sums[f]

        def one(b, carry):
            block_of(b)
            return carry

        block_of(0, first=True)
        lax.fori_loop(1, CY // 4 - 1, one, 0)
        block_of(CY // 4 - 1, last=True)

    def residual_edges(p, k):
        for f in range(2):
            for side, b in ((0, 0), (1, CY // 4 - 1)):
                pad = slice(0, 8) if side == 0 else slice(ROWS + 8, PAD)
                rows = pl.ds(f * 128 + b, 8, stride=12)
                rbuf[rows, :] += sum(face_y[side, t] * xs[p][f, t, pad] for t in range(T))
        for f in range(2):
            for side in range(2):
                prods[f, side] = face_x[side] * hx[k, side, f]
        for f in range(2):
            for side, start in ((0, f * 128), (1, f * 128 + 84)):
                rbuf[start:start + 12, :] += sum(prods[f, side, pl.ds(j, 12, stride=4), :] for j in range(4))

    def send_to(i, src, dst, send, recv):
        other, device = peer(i)
        pltpu.make_async_remote_copy(
            src.at[other], dst.at[me], send, recv, device_id=device, device_id_type=MESH
        ).start()

    def send_all(src, dst, send, recv):
        def one(i, carry):
            for j in range(7):
                send_to(7 * i + j + 1, src, dst, send, recv)
            return carry

        lax.fori_loop(0, (n - 2) // 7, one, 0)
        for i in range((n - 2) // 7 * 7 + 1, n):
            send_to(i, src, dst, send, recv)

    def keep(src, dst, recv):
        pltpu.make_async_copy(src.at[me], dst.at[me], recv).start()

    def sent(src, send):
        pltpu.make_async_copy(src.at[0:n - 1], src.at[0:n - 1], send).wait()

    def received(dst, recv):
        pltpu.make_async_copy(dst, dst, recv).wait()

    def coarse(cycle):
        gbuf[...] = jnp.dot(p_out[...], rbuf[...].astype(BF16), preferred_element_type=F32)

        def pack(i, carry):
            rows = gbuf[pl.ds(pl.multiple_of(i * 8, 8), 8), :].astype(BF16)
            send_a[cycle, 2 * i] = rows[0:4]
            send_a[cycle, 2 * i + 1] = rows[4:8]
            return carry

        lax.fori_loop(0, n // 2, pack, 0, unroll=4)
        keep(send_a.at[cycle], recv_a.at[cycle], a_r.at[me])
        send_all(send_a.at[cycle], recv_a.at[cycle], a_s, a_r.at[me])
        if cycle == 0:
            mats_copy.wait()
        first_slot = lax.broadcasted_iota(jnp.int32, (4, CZ), 0) < 2

        def answer(steps):
            sources = [lax.rem(me - i + n, n) for i in steps]
            for source in sources:
                rows = recv_a.at[cycle, source]
                pltpu.make_async_copy(rows, rows, a_r.at[source]).wait()
            for source in sources:
                both = mats[pl.ds(2 * source, 2)].reshape(2 * CZ, CZ)
                product = lax.dot_general(recv_a[cycle, source], both, CONTRACT_LAST, preferred_element_type=F32)
                send_b[cycle, source] = jnp.where(first_slot, product[:, :CZ], product[:, CZ:])

        def reply(i):
            source = lax.rem(me - i + n, n)
            device = (lax.div(source, ny), lax.rem(source, ny))
            pltpu.make_async_remote_copy(
                send_b.at[cycle, source], recv_b.at[cycle, me], b_s, b_r, device_id=device, device_id_type=MESH
            ).start()

        answer([0])
        keep(send_b.at[cycle], recv_b.at[cycle], b_r)

        def some(i, carry):
            steps = [7 * i + j + 1 for j in range(7)]
            answer(steps)
            for step in steps:
                reply(step)
            return carry

        lax.fori_loop(0, (n - 2) // 7, some, 0)
        rest = list(range((n - 2) // 7 * 7 + 1, n))
        answer(rest)
        for step in rest:
            reply(step)
        sent(send_a.at[cycle], a_s)
        received(recv_b.at[cycle], b_r)
        sent(send_b.at[cycle], b_s)

        def unpack(i, carry):
            gbuf[pl.ds(pl.multiple_of(i * 8, 8), 8), :] = jnp.concatenate(
                [recv_b[cycle, 2 * i], recv_b[cycle, 2 * i + 1]], axis=0
            )
            return carry

        lax.fori_loop(0, n // 2, unpack, 0, unroll=4)
        rows = gbuf[...]
        high = rows.astype(BF16)
        low = (rows - high.astype(F32)).astype(BF16)
        cbuf[...] = jnp.dot(p_in[...], high, preferred_element_type=F32) + jnp.dot(
            p_in[...], low, preferred_element_type=F32
        )

    def correct_edges(p, k):
        q = 1 - p
        for f in range(2):
            for y, b in ((0, 0), (CY - 1, CY // 4 - 1)):
                extra = cbuf[pl.ds(f * 128 + b, 8, stride=12), :]
                for t in range(T):
                    xs[q][f, t, y * 8 + 8:y * 8 + 16] = xs[p][f, t, y * 8 + 8:y * 8 + 16] + extra
            for block in range(CY // 8):
                for side, t, s in ((0, 0, 0), (1, T - 1, 7)):
                    at = f * 128 + s * 12 + block * 2
                    extra = jnp.where(
                        sub8 < 4,
                        jnp.broadcast_to(cbuf[at:at + 1], (8, CZ)),
                        jnp.broadcast_to(cbuf[at + 1:at + 2], (8, CZ)),
                    )
                    rows = pl.ds(8 + block * 64 + s, 8, stride=8)
                    sx[k, side, f, block * 8:block * 8 + 8] = xs[p][f, t, rows, :] + extra

    def correct(p):
        q = 1 - p

        def block_of(b, js):
            for f in range(2):
                extra = cbuf[pl.ds(f * 128 + b, 8, stride=12), :]
                for j in js:
                    for t in range(T):
                        rows = pl.ds(pl.multiple_of((b * 4 + j) * 8 + 8, 8), 8)
                        xs[q][f, t, rows, :] = xs[p][f, t, rows, :] + extra

        def one(b, carry):
            block_of(b, range(4))
            return carry

        block_of(0, (1, 2, 3))
        lax.fori_loop(1, CY // 4 - 1, one, 0)
        block_of(CY // 4 - 1, (0, 1, 2))

    def arrive(copies):
        for copy in copies:
            copy.wait()

    k, p = 0, 0
    moving = exchange(p, k)
    split_edges()
    for cycle in range(CYCLES):
        for step in range(1 if cycle == 0 else 2):
            sweep(p)
            arrive(moving)
            sweep_edges(p, k)
            k, p = k + 1, 1 - p
            moving = exchange(p, k)
        residual(p)
        arrive(moving)
        residual_edges(p, k)
        coarse(cycle)
        k = k + 1
        correct_edges(p, k)
        moving = exchange(1 - p, k)
        correct(p)
        p = 1 - p
        for step in range(2):
            sweep(p)
            arrive(moving)
            sweep_edges(p, k)
            k, p = k + 1, 1 - p
            moving = exchange(p, k)

    arrive(moving)
    for f in range(2):
        xs[p][f, :, 0:8] = xs[p][f, :, 0:8] * in_s
        xs[p][f, :, ROWS + 8:PAD] = xs[p][f, :, ROWS + 8:PAD] * in_n
        hx[k, 0, f] = hx[k, 0, f] * in_w
        hx[k, 1, f] = hx[k, 1, f] * in_e
    for side in range(2):
        hdx[side] = hdx[side] + hx[k, side, 0]

    def update(i, carry):
        row = pl.multiple_of(i * 8, 8)
        for t in range(T):
            hl[t, pl.ds(row, 8), :] = hl[t, pl.ds(row, 8), :] + xs[p][0, t, pl.ds(row, 8), :]
        return carry

    lax.fori_loop(0, PAD // 8, update, 0)

    def gradient(y, carry):
        for t in range(T):
            h_c, h_all = beside(plain(hl), side_row(hdx, 0), side_row(hdx, 1), t, y, False)
            a_c, a_all = beside(field_of(p, 1), halo_row(k, 0, 1), halo_row(k, 1, 1), t, y, False)
            total = jnp.zeros((8, CZ), F32)
            for h_o, a_o in zip(h_all, a_all):
                total = total + (a_c - a_o) * (h_c - h_o)
            grad[pl.ds(pl.multiple_of(t * ROWS + y * 8, 8), 8), :] = total
        return carry

    lax.fori_loop(0, CY, gradient, 0, unroll=2)

    ones = jnp.ones((8, CZ), BF16)
    for block in range(T):
        cut = slice(block * ROWS, block * ROWS + ROWS)
        rows = grad[cut, :]
        high = rows.astype(BF16)
        low = (rows - high.astype(F32)).astype(BF16)
        column = lax.dot_general(ones, high, CONTRACT_LAST, preferred_element_type=F32)
        column = column + lax.dot_general(ones, low, CONTRACT_LAST, preferred_element_type=F32)
        column = column[0:1] * (-0.5 / CZ)
        high = column.astype(BF16).astype(F32)
        low = column - high
        mine = lax.broadcasted_iota(jnp.int32, (n, ROWS), 0).astype(F32) == zone_dev[:, cut]
        parts = jnp.zeros((n, ZDEV), F32)
        for value in (high, low):
            spread = jnp.where(mine, value, 0.0).astype(BF16)
            parts = parts + lax.dot_general(spread, zone_hot[:, cut], CONTRACT_LAST, preferred_element_type=F32)
        if block == 0:
            lz[...] = parts
        else:
            lz[...] += parts

    def pack_zones(i, carry):
        rows = lz[pl.ds(pl.multiple_of(i * 8, 8), 8), :]
        for j in range(8):
            send_z[8 * i + j] = rows[j:j + 1]
        return carry

    lax.fori_loop(0, n // 8, pack_zones, 0)
    keep(send_z, recv_z, z_r)
    send_all(send_z, recv_z, z_s, z_r)

    def natural(t, carry):
        for s in range(8):
            for block in range(CY // 8):
                onat[4 * s + t, block * 8:block * 8 + 8, :] = hl[t, pl.ds(8 + block * 64 + s, 8, stride=8), :]
        return carry

    lax.fori_loop(0, T, natural, 0)
    out_copy = pltpu.make_async_copy(onat, out_head, out_sem)
    out_copy.start()
    received(recv_z, z_r)
    sent(send_z, z_s)

    def add_zones(i, total):
        return total + recv_z[i]

    out_zone[...] = lax.fori_loop(0, n, add_zones, jnp.zeros((1, ZDEV), F32), unroll=8)
    out_copy.wait()


def on_device(
    head, conductivity, storage, recharge, misfit, reservoir_cell, pumping, observed, tile_owner, tile_inverse, zone_of_column
):
    nx, ny = lax.axis_size("gx"), lax.axis_size("gy")
    n = nx * ny
    zone = jnp.transpose(zone_of_column.reshape(8, T, CY), (1, 2, 0)).reshape(1, CX * CY)
    anywhere, vmem = pl.BlockSpec(memory_space=pl.ANY), pl.BlockSpec(memory_space=pltpu.VMEM)
    dma = pltpu.SemaphoreType.DMA
    new_head, zones = pl.pallas_call(
        functools.partial(kernel, nx, ny),
        out_shape=(
            jax.ShapeDtypeStruct((CX, CY, CZ), F32),
            jax.ShapeDtypeStruct((1, ZDEV), F32),
        ),
        in_specs=[anywhere] * 5 + [vmem] * 4 + [anywhere, vmem],
        out_specs=(anywhere, vmem),
        scratch_shapes=[
            pltpu.VMEM((5, CX, CY, CZ), F32),
            pltpu.VMEM((2 * n, CZ, CZ), BF16),
            pltpu.VMEM((T, PAD, CZ), F32),
            pltpu.VMEM((T, PAD, CZ), F32),
            pltpu.VMEM((2, CY, CZ), F32),
            pltpu.VMEM((2, CY, CZ), F32),
            pltpu.VMEM((6, T, ROWS, CZ), F32),
            pltpu.VMEM((T, ROWS, CZ), F32),
            pltpu.VMEM((2, T, ROWS, CZ), F32),
            pltpu.VMEM((2, T, PAD, CZ), F32),
            pltpu.VMEM((2, T, PAD, CZ), F32),
            pltpu.VMEM((EXCHANGES, 2, 2, CY, CZ), F32),
            pltpu.VMEM((EXCHANGES, 2, 2, CY, CZ), F32),
            pltpu.VMEM((2, CY, CZ), F32),
            pltpu.VMEM((2, CY, CZ), F32),
            pltpu.VMEM((2, T, 8, CZ), F32),
            pltpu.VMEM((2, T, 8, CZ), F32),
            pltpu.VMEM((2, 2, CY, CZ), F32),
            pltpu.VMEM((CX * CY, CZ), F32),
            pltpu.VMEM((CX, CY, CZ), F32),
            pltpu.VMEM((1, 128), F32),
            pltpu.VMEM((4 * n, 256), BF16),
            pltpu.VMEM((256, 4 * n), BF16),
            pltpu.VMEM((ZDEV, CX * CY), BF16),
            pltpu.VMEM((256, CZ), F32),
            pltpu.VMEM((4 * n, CZ), F32),
            pltpu.VMEM((256, CZ), F32),
            pltpu.VMEM((CYCLES, n, 4, CZ), BF16),
            pltpu.VMEM((CYCLES, n, 4, CZ), BF16),
            pltpu.VMEM((CYCLES, n, 4, CZ), F32),
            pltpu.VMEM((CYCLES, n, 4, CZ), F32),
            pltpu.VMEM((n, ZDEV), F32),
            pltpu.VMEM((n, 1, ZDEV), F32),
            pltpu.VMEM((n, 1, ZDEV), F32),
            dma((5,)), dma, dma, dma((8,)), dma((8,)), dma((EXCHANGES, 4)), dma((EXCHANGES, 4)),
            dma, dma((n,)), dma, dma, dma, dma,
        ],
        compiler_params=pltpu.CompilerParams(
            collective_id=0, has_side_effects=True, vmem_limit_bytes=60 * 1024 * 1024
        ),
        name="newton",
    )(
        head, conductivity, storage, recharge, misfit, reservoir_cell.reshape(1, -1), pumping.reshape(1, -1),
        observed.reshape(1, -1), tile_owner.reshape(1, -1), tile_inverse, zone,
    )
    return new_head, zones.reshape(ZDEV)


def solution(mesh):
    block, flat = P("gx", "gy", None), P(("gx", "gy"))
    placed = (block,) * 5 + (flat,) * 3 + (P(("gx", "gy"), None), P(("gx", "gy"), None, None), P("gx", "gy"))
    return jax.shard_map(
        on_device, mesh=mesh, in_specs=placed, out_specs=(block, flat), check_vma=False
    )
```
